32 devices in a mesh: grp: 2 (over x), pi: 16 (over z, y, core).
Axes of the slice: x: 2, y: 2, z: 4, core: 2. Of those that a mesh axis runs over, the one named last changes fastest.
Arguments:
- left: bfloat16 [128, 1024], P(('grp', 'pi')), parts along dimension 0, may hold values from -6 to 6
- right: bfloat16 [128, 1024], P(('grp', 'pi')), parts along dimension 0, may hold values from -6 to 6
- depth: int32 [128], P(('grp', 'pi')), parts along dimension 0, may hold values from 1 to 32
- w_out: bfloat16 [1024, 128], replicated, may hold values from -0.1875 to 0.1875
- bias: float32 [128], replicated, may hold values from -4 to 4
- pair_cot: bfloat16 [128, 64, 128], P(('grp', 'pi')), parts along dimension 0, may hold values from -6 to 6
Outputs:
- pair_update: bfloat16 [128, 64, 128], P(('grp', 'pi')), parts along dimension 0
- grad_left: float32 [128, 1024], P(('grp', 'pi')), parts along dimension 0
- grad_right: float32 [128, 1024], P(('grp', 'pi')), parts along dimension 0
- grad_w: float32 [2048, 128], P('grp'), parts along dimension 0
- grad_bias: float32 [256], P('grp'), parts along dimension 0
The draws below stay inside these ranges and needn't reach their ends.
There are 2 independent parts, one for each index of `grp`. The reference program is written for one: setup_inputs(seed, part) draws one part's arguments, and reference() takes and returns one part's arrays. A program takes and returns all parts, laid end to end along the dimension named above; an argument that names none is the same for every part. Nothing has to cross between parts.
All inputs are finite; a program needn't handle non-finite values.
Results may differ from the reference program's by a relative error of at most 0.0034.
Values may be sent and summed in bfloat16 or wider, within the bound.
A program may use at most 64 MiB of HBM per device.

```python
import math
import jax
import jax.numpy as jnp
from jax import lax

C = 32
CZ = 128
ROWS = 32
N = 64


def with_ends(drawn, key, least, largest):
    longest = drawn.shape.index(max(drawn.shape))
    spots = []
    for shift in (0, 1):
        where = [jax.random.randint(jax.random.fold_in(key, axis), (), 0, length) for axis, length in enumerate(drawn.shape)]
        where[longest] = (where[longest] + shift) % drawn.shape[longest]
        spots.append(tuple(where))
    return drawn.at[spots[0]].set(least).at[spots[1]].set(largest)


def raised(drawn, stream_key, source, target, shards_of, factor):
    def block_of(axis_at):
        return (jnp.arange(drawn.shape[axis_at]) // (drawn.shape[axis_at] // shards_of)).reshape((-1,) + (1,) * (drawn.ndim - 1 - axis_at))

    first = jax.random.permutation(stream_key, shards_of)[block_of(target)]
    second = (block_of(target) + shards_of // 2) % shards_of
    return jnp.where((block_of(source) == first) | (block_of(source) == second), factor * drawn, drawn)


def levels(stream_key, extent, pieces, smallest, high):
    gain = 1.0
    for dim, blocks in pieces:
        draws = jax.random.uniform(jax.random.fold_in(jax.random.fold_in(stream_key, 6), dim), (blocks,), jnp.float32, smallest / len(pieces), high / len(pieces))
        gain = gain * jnp.repeat(jnp.exp(draws), extent[dim] // blocks).reshape((-1,) + (1,) * (len(extent) - 1 - dim))
    return gain


def bell_draw(own_key, extent, width, most, split=(), held_as=jnp.bfloat16):
    drawn = jax.random.normal(own_key, extent, jnp.float32) * width
    if len(split) > 0:
        drawn = levels(own_key, extent, split, -0.22, 0.18) * drawn
    return jnp.clip(drawn, min=-most, max=most).astype(held_as)


def noise_with(rng, extent, scale, reach, shards, heavy, kind=jnp.bfloat16):
    entries = scale * jax.random.normal(rng, extent, jnp.float32)
    if shards:
        entries = entries * levels(rng, extent, shards, -0.22, 0.18)
    return jnp.clip(raised(entries, jax.random.fold_in(rng, 3), *heavy), -reach, reach).astype(kind)


def setup_inputs(seed: int = 0, part: int = 0) -> dict:
    arg_keys = jax.random.split(jax.random.key(seed), 7)
    part_splits = jax.random.split(jax.random.fold_in(arg_keys[6], part), 7)
    return {
        "left": bell_draw(part_splits[0], (N, ROWS * C), 1.0, 6.0, ((0, 16),)),
        "right": bell_draw(part_splits[1], (N, ROWS * C), 1.0, 6.0, ((0, 16),)),
        "depth": with_ends(jax.random.randint(part_splits[2], (N,), 1, ROWS + 1), jax.random.fold_in(part_splits[2], 1), 1, ROWS).astype(jnp.int32),
        "w_out": bell_draw(arg_keys[3], (C * C, CZ), (C * C) ** -0.5, 0.1875),
        "bias": bell_draw(arg_keys[4], (CZ,), 1.0, 4.0, (), jnp.float32),
        "pair_cot": noise_with(part_splits[5], (N, N, CZ), 1.0, 6.0, ((0, 16),), (0, 1, 16, 2.0)),
    }


epsilon = 1e-3


def reference(left, right, depth, w_out, bias, pair_cot):
    row_ids = jnp.arange(ROWS, dtype=jnp.int32)
    mask = (row_ids[None, :] < depth[:, None]).astype(jnp.bfloat16)
    left_masked = left.reshape(N, ROWS, C) * mask[:, :, None]
    right_masked = right.reshape(N, ROWS, C) * mask[:, :, None]
    block = math.gcd(N, 32)
    blocks = N // block

    def one_block(carry, block_index):
        weight_acc, bias_acc, right_acc = carry
        begin = (block_index * block).astype(jnp.int32)
        left_block = lax.dynamic_slice_in_dim(left_masked, begin, block, 0)
        depth_block = lax.dynamic_slice_in_dim(depth, begin, block, 0)
        mask_block = lax.dynamic_slice_in_dim(mask, begin, block, 0)
        cot_block = lax.dynamic_slice_in_dim(pair_cot, begin, block, 0)
        count = epsilon + jnp.minimum(depth_block[:, None], depth[None, :]).astype(jnp.float32)
        outer = jnp.einsum("isc,jsd->ijcd", left_block.astype(jnp.float32), right_masked.astype(jnp.float32))
        outer = (outer / count[:, :, None, None]).reshape(block, N, C * C).astype(jnp.bfloat16)
        update = (jnp.dot(outer, w_out, preferred_element_type=jnp.float32) + bias).astype(jnp.bfloat16)
        weight_acc = weight_acc + jnp.dot(outer.reshape(-1, C * C).T, cot_block.reshape(-1, CZ), preferred_element_type=jnp.float32)
        bias_acc = bias_acc + jnp.sum(cot_block, axis=(0, 1), dtype=jnp.float32)
        grad_pair = jnp.dot(cot_block, w_out.T, preferred_element_type=jnp.float32) / count[:, :, None]
        grad_pair = grad_pair.astype(jnp.bfloat16).reshape(block, N, C, C).astype(jnp.float32)
        left_grad = jnp.einsum("ijcd,jsd->isc", grad_pair, right_masked.astype(jnp.float32)) * mask_block[:, :, None]
        right_acc = right_acc + jnp.einsum("ijcd,isc->jsd", grad_pair, left_block.astype(jnp.float32))
        return (weight_acc, bias_acc, right_acc), (update, left_grad)

    init = (jnp.zeros((C * C, CZ), jnp.float32), jnp.zeros((CZ,), jnp.float32), jnp.zeros((N, ROWS, C), jnp.float32))
    carry, stacked = lax.scan(one_block, init, jnp.arange(blocks, dtype=jnp.int32))
    weight_acc, bias_acc, right_acc = carry
    updates, left_grads = stacked
    pair_update = updates.reshape(N, N, CZ)
    grad_left = left_grads.reshape(N, ROWS * C)
    grad_right = (right_acc * mask[:, :, None]).reshape(N, ROWS * C)
    return pair_update, grad_left, grad_right, weight_acc, bias_acc
```

```python
import functools

import jax
import jax.numpy as jnp
from jax import lax
from jax.experimental import pallas as pl
from jax.experimental.pallas import tpu as pltpu
from jax.sharding import PartitionSpec as P

C = 32
LOW = 8
EPSILON = 0.001
MESH = pl.DeviceIdType.MESH
F32 = jnp.float32
BF16 = jnp.bfloat16
I32 = jnp.int32


def split(x):
    high = x.astype(BF16)
    return high, (x - high.astype(F32)).astype(BF16)


def mm(x, y):
    return jnp.dot(x, y, preferred_element_type=F32)


def mm_nt(x, y):
    return lax.dot_general(x, y, (((1,), (1,)), ((), ())), preferred_element_type=F32)


def iota(shape, axis):
    return lax.broadcasted_iota(I32, shape, axis)


def one_hot(hit):
    return hit.astype(F32).astype(BF16)


def kernel(
    n, left_in, right_in, depth_in, cot_in, w_in, bias_in,
    pu_ref, gl_ref, gr_ref, gw_ref, gb_ref,
    left_v, right_v, depth_v, cot_v, w_v, bias_v,
    xs, gat, xl, lf, b_t, w_ref, o_ref, g_raw, g_ref, send_w, own_w, recv_w, mine_w, all_w,
    send_r, recv_r, r_t, pu_part, pu_got, gl_part, gl_got,
    local_sems, send_sems, recv_sems, ag_sems,
):
    me = lax.axis_index("pi")
    rows, width = right_v.shape
    z = w_v.shape[1]
    samples = width // C
    total = cot_v.shape[2]
    chips = n // 2
    core = lax.rem(me, 2)
    chip = me // 2
    partner = me + 1 - 2 * core
    half = C // 2
    block = LOW * C
    highs = samples // LOW
    part = half * LOW
    q = highs * part
    pairs = rows
    lanes = 2 * total
    chunk = own_w.shape[1]

    bits = [1 << k for k in range((n - 1).bit_length())]
    mine = [lax.rem(me // v, 2) for v in bits]

    def peer(x):
        where = 0
        for v, own in zip(bits, mine):
            where = where + v * lax.rem(own + (x // v) % 2, 2)
        return where

    def each(act, start, stop, step):
        if n <= 32:
            for x in range(start, stop, step):
                act(peer(x))
        else:
            def body(t, carry):
                act(peer(start + step * t))
                return carry

            lax.fori_loop(0, len(range(start, stop, step)), body, 0)

    def everyone(act):
        each(act, n - 1, 0, -1)

    def alike(act):
        each(act, n - 2, 0, -2)

    def copy(k, source, target, p, recv=None):
        return pltpu.make_async_remote_copy(
            src_ref=source, dst_ref=target,
            send_sem=send_sems.at[k], recv_sem=recv_sems.at[k] if recv is None else recv,
            device_id={"pi": p}, device_id_type=MESH,
        )

    def fetch(k, source, target):
        return pltpu.make_async_copy(source, target, local_sems.at[k])

    fetches = [
        fetch(0, right_in, right_v), fetch(1, depth_in, depth_v), fetch(2, cot_in, cot_v.at[core]),
        fetch(3, left_in, left_v), fetch(4, w_in, w_v), fetch(5, bias_in, bias_v),
    ]
    for f in fetches:
        f.start()
    barrier = pltpu.get_barrier_semaphore()
    everyone(
        lambda p: pl.semaphore_signal(barrier, inc=1, device_id={"pi": p}, device_id_type=MESH)
    )

    perm = one_hot(
        (iota((block, block), 0) % C == iota((block, block), 1) // LOW)
        & (iota((block, block), 0) // C == iota((block, block), 1) % LOW)
    )
    fetches[0].wait()
    fetches[1].wait()
    spot = (rows, rows)
    wide = jnp.broadcast_to(depth_v[...], spot).astype(F32)
    own_depth = jnp.sum(
        jnp.where(iota(spot, 0) == iota(spot, 1), wide, 0.0), axis=1, keepdims=True
    )
    kept = (iota((rows, width), 1) // C).astype(F32) < jnp.broadcast_to(own_depth, (rows, width))
    right = jnp.where(kept, right_v[...].astype(F32), 0.0)
    stacked = jnp.concatenate([right[:, h * block:(h + 1) * block] for h in range(highs)], axis=0)
    moved = mm(stacked.astype(BF16), perm)
    for k in range(2):
        for h in range(highs):
            xs[k, :, h * part:(h + 1) * part] = (
                moved[h * rows:(h + 1) * rows, k * part:(k + 1) * part].astype(BF16)
            )
    fetches[2].wait()
    cot_sum = jnp.zeros((1, z), F32)
    for i in range(rows):
        cot_sum = cot_sum + jnp.sum(cot_v[core, i].astype(F32), axis=0, keepdims=True)
    high, low = split(cot_sum)
    spread = jnp.where(
        iota((rows, lanes), 1) % total == me * rows + iota((rows, lanes), 0),
        jnp.broadcast_to(own_depth, (rows, lanes)), 0.0,
    )
    places = jnp.sum(spread, axis=0, keepdims=True)
    parts = [high.astype(F32), low.astype(F32)]
    if lanes > z:
        parts = [jnp.concatenate([v, jnp.zeros((1, lanes - z), F32)], axis=1) for v in parts]
    extra = jnp.concatenate(parts + [places, jnp.zeros((rows - 3, lanes), F32)], axis=0).astype(BF16)
    for k in range(2):
        xs[k, :, q:] = extra
    fetches[3].wait()
    xl[core, :, :width] = jnp.where(kept, left_v[...].astype(F32), 0.0).astype(BF16)
    xl[core, :, width:] = jnp.broadcast_to(own_depth, (rows, z)).astype(BF16)
    gat[me] = xs[core]

    pl.semaphore_wait(barrier, n - 1)
    everyone(lambda p: copy(0, xs.at[lax.rem(p, 2)], gat.at[me], p).start())
    left_copy = copy(1, xl.at[core], xl.at[core], partner)
    cot_copy = copy(2, cot_in, cot_v.at[core], partner)
    left_copy.start()
    cot_copy.start()

    fetches[4].wait()
    fetches[5].wait()
    turned = one_hot(
        (iota((part, block), 1) % C == iota((part, block), 0) // LOW + half * core)
        & (iota((part, block), 1) // C == iota((part, block), 0) % LOW)
    )
    settle = one_hot(
        (iota((part, part), 1) // LOW == iota((part, part), 0) % half)
        & (iota((part, part), 1) % LOW == iota((part, part), 0) // half)
    )
    tops = C // LOW
    moved_w = mm(turned, jnp.concatenate([w_v[t * block:(t + 1) * block] for t in range(tops)], axis=1))
    w_half = jnp.concatenate(
        [moved_w[d * LOW:(d + 1) * LOW, t * z:(t + 1) * z] for d in range(half) for t in range(tops)],
        axis=0,
    )
    w_own = w_half.astype(BF16)
    w_t = w_half.T.astype(BF16)

    left_copy.wait_recv()
    for k in range(2):
        lf[k * rows:(k + 1) * rows] = xl[k].astype(F32)
    diagonal = iota((LOW, block), 1) // C == iota((LOW, block), 0)
    lines = [
        jnp.where(
            diagonal, jnp.broadcast_to(lf[i:i + 1, h * block:(h + 1) * block], (LOW, block)), 0.0
        )
        for i in range(2 * rows) for h in range(highs)
    ]
    fold = one_hot(iota((block, pairs * C), 0) % C == iota((block, pairs * C), 1) % C)
    folded = mm(jnp.concatenate(lines, axis=0).astype(BF16), fold)
    place = iota((samples, pairs * C), 1) // C
    pieces = []
    for i2 in range(2):
        piece = jnp.zeros((samples, pairs * C), F32)
        for p in range(pairs):
            at = (2 * p + i2) * samples
            piece = jnp.where(place == p, folded[at:at + samples], piece)
        pieces.append(piece)
    a_full = jnp.concatenate(pieces, axis=0)
    a = a_full.astype(BF16)
    a_t = a_full.T.astype(BF16)
    first = iota((1, lanes), 1) < total
    own_lanes = [
        jnp.where(
            first,
            jnp.broadcast_to(lf[2 * p:2 * p + 1, width:width + 1], (1, lanes)),
            jnp.broadcast_to(lf[2 * p + 1:2 * p + 2, width:width + 1], (1, lanes)),
        )
        for p in range(pairs)
    ]

    cot_copy.wait_recv()
    cot = cot_v[...].reshape(2 * rows * total, z)
    g_raw[...] = mm_nt(w_own, cot)

    copy(0, gat.at[pl.ds(0, n - 1)], gat.at[pl.ds(0, n - 1)], partner).wait_recv()
    ext = jnp.zeros((rows, lanes), F32)
    for p in range(n):
        ext = ext + gat[p, :, q:].astype(F32)
    gb_ref[...] = ext[0:1, :z] + ext[1:2, :z]
    inverse = [1.0 / (EPSILON + jnp.minimum(ext[2:3], own_lanes[p])) for p in range(pairs)]
    b = jnp.concatenate([gat[p, :, :q].astype(F32) for p in range(n)], axis=0)
    b_t[...] = jnp.concatenate([b, b], axis=0).T
    in_first = iota((samples, lanes), 1) < total
    for d in range(half):
        rows_d = jnp.concatenate(
            [b_t[h * part + d * LOW:h * part + (d + 1) * LOW] for h in range(highs)], axis=0
        )
        w_ref[:samples, d * lanes:(d + 1) * lanes] = jnp.where(in_first, rows_d, 0.0).astype(BF16)
        w_ref[samples:, d * lanes:(d + 1) * lanes] = jnp.where(in_first, 0.0, rows_d).astype(BF16)
    for d in range(0, half, 2):
        product = mm(a_t, w_ref[:, d * lanes:(d + 2) * lanes])
        for e in range(2):
            for p in range(pairs):
                o_ref[(d + e) * C:(d + e + 1) * C, p * lanes:(p + 1) * lanes] = (
                    product[p * C:(p + 1) * C, e * lanes:(e + 1) * lanes] * inverse[p]
                ).astype(BF16)
    gw = mm(o_ref[...], cot)
    gw = jnp.concatenate(
        [
            jnp.concatenate([gw[d * C + t * LOW:d * C + (t + 1) * LOW] for d in range(half)], axis=0)
            for t in range(tops)
        ],
        axis=1,
    )
    gw = mm(settle, gw.astype(BF16))
    for t in range(tops):
        send_w[t * part:(t + 1) * part] = gw[:, t * z:(t + 1) * z].astype(BF16)

    def chunk_of(m):
        return pl.ds(pl.multiple_of(m * chunk, chunk), chunk)

    alike(lambda p: copy(3, send_w.at[chunk_of(p // 2)], recv_w.at[chip], p).start())

    for d in range(half):
        for p in range(pairs):
            g_ref[p * C:(p + 1) * C, d * lanes:(d + 1) * lanes] = (
                g_raw[d * C:(d + 1) * C, p * lanes:(p + 1) * lanes] * inverse[p]
            ).astype(BF16)
    for d in range(0, half, 2):
        product = mm(a, g_ref[:, d * lanes:(d + 2) * lanes])
        for e in range(2):
            view = product[:, e * lanes:(e + 1) * lanes]
            chosen = jnp.where(in_first, view[:samples], view[samples:])
            for h in range(highs):
                r_t[h, (d + e) * LOW:(d + e + 1) * LOW] = chosen[h * LOW:(h + 1) * LOW]
    for h in range(highs):
        flat = r_t[h].T
        flat = (flat[:total] + flat[total:]).astype(BF16)
        for p in range(n):
            send_r[p, :, h * part:(h + 1) * part] = flat[p * rows:(p + 1) * rows]
    everyone(lambda p: copy(4, send_r.at[p], recv_r.at[me], p).start())
    recv_r[me] = send_r[me]

    left_sum = mm_nt(g_ref[...], w_ref[...])
    tall = rows * C // 2
    for k in range(2):
        gl_part[k] = left_sum[k * tall:(k + 1) * tall]
    gl_copy = copy(5, gl_part.at[1 - core], gl_got, partner)
    gl_copy.start()

    update = mm(w_t, o_ref[...])
    for p in range(pairs):
        flat = update[:, p * lanes:(p + 1) * lanes].T
        for e in range(2):
            i = 2 * p + e
            pu_part[i // rows, i % rows] = flat[e * total:(e + 1) * total]
    pu_copy = copy(6, pu_part.at[1 - core], pu_got, partner)
    pu_copy.start()

    own_chunk = send_w[chunk_of(chip)].astype(F32)
    all_recv = copy(3, send_w.at[pl.ds(0, (chips - 1) * chunk)], send_w.at[pl.ds(0, (chips - 1) * chunk)], partner)
    recv_w[chip] = jnp.zeros((chunk, z), BF16)
    all_recv.wait_recv()
    total_w = own_chunk
    for m in range(chips):
        total_w = total_w + recv_w[m].astype(F32)
    mine_w[...] = total_w.astype(BF16)

    def direct(p):
        return copy(7, mine_w, all_w.at[core, chip], p, ag_sems.at[chip])

    def landed(p):
        return copy(8, all_w.at[core, p // 2], all_w.at[core, p // 2], partner)

    alike(lambda p: direct(p).start())
    copy(8, mine_w, all_w.at[core, chip], partner).start()
    all_w[core, chip] = mine_w[...]

    gl_copy.wait_recv()
    owned = gl_part[core] + gl_got[...]
    owned = owned.T
    high, low = split(owned)
    unfold = one_hot(
        (iota((pairs * C // 2, pairs // 2 * block), 0) % C == iota((pairs * C // 2, pairs // 2 * block), 1) % C)
        & (iota((pairs * C // 2, pairs // 2 * block), 0) // C == iota((pairs * C // 2, pairs // 2 * block), 1) // block)
    )
    opened = mm(high, unfold) + mm(low, unfold)
    for p in range(pairs // 2):
        for i2 in range(2):
            for h in range(highs):
                at = i2 * samples + h * LOW
                view = opened[at:at + LOW, p * block:(p + 1) * block]
                gl_ref[2 * p + i2:2 * p + i2 + 1, h * block:(h + 1) * block] = jnp.sum(
                    jnp.where(diagonal, view, 0.0), axis=0, keepdims=True
                )
    gl_ref[...] = jnp.where(kept, gl_ref[...], 0.0)

    pu_copy.wait_recv()
    for i in range(rows):
        pu_ref[i] = (pu_part[core, i] + pu_got[i] + bias_v[...]).astype(BF16)

    copy(4, send_r.at[pl.ds(0, n - 1)], recv_r.at[pl.ds(0, n - 1)], partner).wait_recv()
    sums = []
    for k in range(2):
        acc = jnp.zeros((rows, q), F32)
        for m in range(chips):
            acc = acc + recv_r[2 * m + k].astype(F32)
        sums.append(acc)
    joined = jnp.concatenate(
        [
            jnp.concatenate([sums[k][:, h * part:(h + 1) * part] for k in range(2)], axis=1)
            for h in range(highs)
        ],
        axis=0,
    )
    high, low = split(joined)
    natural = mm_nt(high, perm) + mm_nt(low, perm)
    natural = jnp.concatenate([natural[h * rows:(h + 1) * rows] for h in range(highs)], axis=1)
    gr_ref[...] = jnp.where(kept, natural, 0.0)

    def forward(p):
        pltpu.make_async_remote_copy(
            src_ref=mine_w, dst_ref=all_w.at[core, p // 2],
            send_sem=send_sems.at[7], recv_sem=ag_sems.at[p // 2],
            device_id={"pi": partner}, device_id_type=MESH,
        ).wait_recv()
        landed(p).start()

    each(forward, 2, n, 2)
    copy(8, all_w.at[1 - core], all_w.at[1 - core], partner).wait_recv()
    gw_ref[...] = all_w[...]

    copy(0, gat.at[pl.ds(0, n - 1)], gat.at[pl.ds(0, n - 1)], partner).wait_send()
    left_copy.wait_send()
    cot_copy.wait_send()
    all_recv.wait_send()
    copy(4, send_r.at[pl.ds(0, n - 1)], recv_r.at[pl.ds(0, n - 1)], partner).wait_send()
    gl_copy.wait_send()
    pu_copy.wait_send()
    copy(7, send_w.at[pl.ds(0, (chips - 1) * chunk)], send_w.at[pl.ds(0, (chips - 1) * chunk)], partner).wait_send()
    copy(8, all_w.at[core], all_w.at[core], partner).wait_send()


def finish(pu, gl, gr, gw, gb, pu_out, gl_out, gr_out, gw_out, gb_out):
    pu_out[...] = pu[...]
    gl_out[...] = gl[...]
    gr_out[...] = gr[...]
    gb_out[...] = gb[...]
    half = C // 2
    for k in range(2):
        whole = gw[k].reshape(C * half, gw.shape[-1]).astype(F32)
        for c in range(C):
            gw_out[c * C + k * half:c * C + (k + 1) * half] = whole[c * half:(c + 1) * half]


def local(n, left, right, depth, w_out, bias, pair_cot):
    rows, width = left.shape
    total, z = pair_cot.shape[1:]
    chips = n // 2
    samples = width // C
    q = width // 2
    lanes = 2 * total
    size = C * C // 2
    chunk = size // chips
    vmem = pl.BlockSpec(memory_space=pltpu.VMEM)
    hbm = pl.BlockSpec(memory_space=pl.ANY)
    shapes = (
        jax.ShapeDtypeStruct((rows, total, z), BF16),
        jax.ShapeDtypeStruct((rows, width), F32),
        jax.ShapeDtypeStruct((rows, width), F32),
        jax.ShapeDtypeStruct((2, chips, chunk, z), BF16),
        jax.ShapeDtypeStruct((1, z), F32),
    )
    results = pl.pallas_call(
        functools.partial(kernel, n),
        out_shape=shapes,
        in_specs=[hbm] * 6,
        out_specs=(vmem,) * 5,
        scratch_shapes=[
            pltpu.VMEM((rows, width), BF16),
            pltpu.VMEM((rows, width), BF16),
            pltpu.VMEM((1, rows), jnp.int32),
            pltpu.VMEM((2, rows, total, z), BF16),
            pltpu.VMEM((C * C, z), BF16),
            pltpu.VMEM((1, z), F32),
            pltpu.VMEM((2, rows, q + lanes), BF16),
            pltpu.VMEM((n, rows, q + lanes), BF16),
            pltpu.VMEM((2, rows, width + z), BF16),
            pltpu.VMEM((2 * rows, width + z), F32),
            pltpu.VMEM((q, lanes), F32),
            pltpu.VMEM((2 * samples, C // 2 * lanes), BF16),
            pltpu.VMEM((size, rows * lanes), BF16),
            pltpu.VMEM((size, rows * lanes), F32),
            pltpu.VMEM((rows * C, C // 2 * lanes), BF16),
            pltpu.VMEM((size, z), BF16),
            pltpu.VMEM((1, chunk, z), F32),
            pltpu.VMEM((chips, chunk, z), BF16),
            pltpu.VMEM((chunk, z), BF16),
            pltpu.VMEM((2, chips, chunk, z), BF16),
            pltpu.VMEM((n, rows, q), BF16),
            pltpu.VMEM((n, rows, q), BF16),
            pltpu.VMEM((samples // LOW, C // 2 * LOW, lanes), F32),
            pltpu.VMEM((2, rows, total, z), F32),
            pltpu.VMEM((rows, total, z), F32),
            pltpu.VMEM((2, rows * C // 2, 2 * samples), F32),
            pltpu.VMEM((rows * C // 2, 2 * samples), F32),
            pltpu.SemaphoreType.DMA((6,)),
            pltpu.SemaphoreType.DMA((9,)),
            pltpu.SemaphoreType.DMA((9,)),
            pltpu.SemaphoreType.DMA((chips,)),
        ],
        compiler_params=pltpu.CompilerParams(collective_id=0, has_side_effects=True),
    )(left, right, depth[None, :], pair_cot, w_out, bias[None, :])
    pu, gl, gr, gw, gb = pl.pallas_call(
        finish,
        out_shape=shapes[:3] + (jax.ShapeDtypeStruct((C * C, z), F32),) + shapes[4:],
        in_specs=[vmem] * 5,
        out_specs=(vmem,) * 5,
    )(*results)
    return pu, gl, gr, gw, gb.reshape(z)


def solution(mesh):
    placed = (
        P(("grp", "pi"), None),
        P(("grp", "pi"), None),
        P(("grp", "pi")),
        P(),
        P(),
        P(("grp", "pi"), None, None),
    )
    return jax.shard_map(
        functools.partial(local, mesh.shape["pi"]),
        mesh=mesh,
        in_specs=placed,
        out_specs=(
            P(("grp", "pi"), None, None),
            P(("grp", "pi"), None),
            P(("grp", "pi"), None),
            P("grp", None),
            P("grp"),
        ),
        check_vma=False,
    )
```

```python
import functools

import jax
import jax.numpy as jnp
from jax import lax
from jax.experimental import pallas as pl
from jax.experimental.pallas import tpu as pltpu
from jax.sharding import PartitionSpec as P

C = 32
LOW = 8
EPSILON = 0.001
MESH = pl.DeviceIdType.MESH
F32 = jnp.float32
BF16 = jnp.bfloat16
I32 = jnp.int32


def split(x):
    high = x.astype(BF16)
    return high, (x - high.astype(F32)).astype(BF16)


def mm(x, y):
    return jnp.dot(x, y, preferred_element_type=F32)


def mm_nt(x, y):
    return lax.dot_general(x, y, (((1,), (1,)), ((), ())), preferred_element_type=F32)


def iota(shape, axis):
    return lax.broadcasted_iota(I32, shape, axis)


def one_hot(hit):
    return hit.astype(F32).astype(BF16)


def kernel(
    n, left_in, right_in, depth_in, cot_in, w_in, bias_in,
    pu_ref, gl_ref, gr_ref, gw_ref, gb_ref,
    left_v, right_v, depth_v, cot_v, w_v, bias_v,
    xs, gat, xl, lf, b_t, w_ref, o_ref, g_raw, g_ref, send_w, own_w, recv_w, mine_w, all_w,
    send_r, recv_r, r_t, pu_part, pu_got, gl_part, gl_got,
    local_sems, send_sems, recv_sems, ag_sems,
):
    me = lax.axis_index("pi")
    rows, width = right_v.shape
    z = w_v.shape[1]
    samples = width // C
    total = cot_v.shape[2]
    chips = n // 2
    core = lax.rem(me, 2)
    chip = me // 2
    partner = me + 1 - 2 * core
    half = C // 2
    block = LOW * C
    highs = samples // LOW
    part = half * LOW
    q = highs * part
    pairs = rows
    lanes = 2 * total
    chunk = own_w.shape[1]

    bits = [1 << k for k in range((n - 1).bit_length())]
    mine = [lax.rem(me // v, 2) for v in bits]

    def peer(x):
        where = 0
        for v, own in zip(bits, mine):
            where = where + v * lax.rem(own + (x // v) % 2, 2)
        return where

    def each(act, start, stop, step):
        if n <= 32:
            for x in range(start, stop, step):
                act(peer(x))
        else:
            def body(t, carry):
                act(peer(start + step * t))
                return carry

            lax.fori_loop(0, len(range(start, stop, step)), body, 0)

    def everyone(act):
        each(act, n - 1, 0, -1)

    def alike(act):
        each(act, n - 2, 0, -2)

    def copy(k, source, target, p, recv=None):
        return pltpu.make_async_remote_copy(
            src_ref=source, dst_ref=target,
            send_sem=send_sems.at[k], recv_sem=recv_sems.at[k] if recv is None else recv,
            device_id={"pi": p}, device_id_type=MESH,
        )

    def fetch(k, source, target):
        return pltpu.make_async_copy(source, target, local_sems.at[k])

    fetches = [
        fetch(0, right_in, right_v), fetch(1, depth_in, depth_v), fetch(2, cot_in, cot_v.at[core]),
        fetch(3, left_in, left_v), fetch(4, w_in, w_v), fetch(5, bias_in, bias_v),
    ]
    for f in fetches:
        f.start()
    barrier = pltpu.get_barrier_semaphore()
    everyone(
        lambda p: pl.semaphore_signal(barrier, inc=1, device_id={"pi": p}, device_id_type=MESH)
    )

    perm = one_hot(
        (iota((block, block), 0) % C == iota((block, block), 1) // LOW)
        & (iota((block, block), 0) // C == iota((block, block), 1) % LOW)
    )
    fetches[0].wait()
    fetches[1].wait()
    spot = (rows, rows)
    wide = jnp.broadcast_to(depth_v[...], spot).astype(F32)
    own_depth = jnp.sum(
        jnp.where(iota(spot, 0) == iota(spot, 1), wide, 0.0), axis=1, keepdims=True
    )
    kept = (iota((rows, width), 1) // C).astype(F32) < jnp.broadcast_to(own_depth, (rows, width))
    right = jnp.where(kept, right_v[...].astype(F32), 0.0)
    stacked = jnp.concatenate([right[:, h * block:(h + 1) * block] for h in range(highs)], axis=0)
    moved = mm(stacked.astype(BF16), perm)
    for k in range(2):
        for h in range(highs):
            xs[k, :, h * part:(h + 1) * part] = (
                moved[h * rows:(h + 1) * rows, k * part:(k + 1) * part].astype(BF16)
            )
    fetches[2].wait()
    cot_sum = jnp.zeros((1, z), F32)
    for i in range(rows):
        cot_sum = cot_sum + jnp.sum(cot_v[core, i].astype(F32), axis=0, keepdims=True)
    high, low = split(cot_sum)
    spread = jnp.where(
        iota((rows, lanes), 1) % total == me * rows + iota((rows, lanes), 0),
        jnp.broadcast_to(own_depth, (rows, lanes)), 0.0,
    )
    places = jnp.sum(spread, axis=0, keepdims=True)
    parts = [high.astype(F32), low.astype(F32)]
    if lanes > z:
        parts = [jnp.concatenate([v, jnp.zeros((1, lanes - z), F32)], axis=1) for v in parts]
    extra = jnp.concatenate(parts + [places, jnp.zeros((rows - 3, lanes), F32)], axis=0).astype(BF16)
    for k in range(2):
        xs[k, :, q:] = extra
    fetches[3].wait()
    xl[core, :, :width] = jnp.where(kept, left_v[...].astype(F32), 0.0).astype(BF16)
    xl[core, :, width:] = jnp.broadcast_to(own_depth, (rows, z)).astype(BF16)
    gat[me] = xs[core]

    pl.semaphore_wait(barrier, n - 1)
    everyone(lambda p: copy(0, xs.at[lax.rem(p, 2)], gat.at[me], p).start())
    left_copy = copy(1, xl.at[core], xl.at[core], partner)
    cot_copy = copy(2, cot_in, cot_v.at[core], partner)
    left_copy.start()
    cot_copy.start()

    fetches[4].wait()
    fetches[5].wait()
    turned = one_hot(
        (iota((part, block), 1) % C == iota((part, block), 0) // LOW + half * core)
        & (iota((part, block), 1) // C == iota((part, block), 0) % LOW)
    )
    settle = one_hot(
        (iota((part, part), 1) // LOW == iota((part, part), 0) % half)
        & (iota((part, part), 1) % LOW == iota((part, part), 0) // half)
    )
    tops = C // LOW
    moved_w = mm(turned, jnp.concatenate([w_v[t * block:(t + 1) * block] for t in range(tops)], axis=1))
    w_half = jnp.concatenate(
        [moved_w[d * LOW:(d + 1) * LOW, t * z:(t + 1) * z] for d in range(half) for t in range(tops)],
        axis=0,
    )
    w_own = w_half.astype(BF16)
    w_t = w_half.T.astype(BF16)

    left_copy.wait_recv()
    for k in range(2):
        lf[k * rows:(k + 1) * rows] = xl[k].astype(F32)
    diagonal = iota((LOW, block), 1) // C == iota((LOW, block), 0)
    lines = [
        jnp.where(
            diagonal, jnp.broadcast_to(lf[i:i + 1, h * block:(h + 1) * block], (LOW, block)), 0.0
        )
        for i in range(2 * rows) for h in range(highs)
    ]
    fold = one_hot(iota((block, pairs * C), 0) % C == iota((block, pairs * C), 1) % C)
    folded = mm(jnp.concatenate(lines, axis=0).astype(BF16), fold)
    place = iota((samples, pairs * C), 1) // C
    pieces = []
    for i2 in range(2):
        piece = jnp.zeros((samples, pairs * C), F32)
        for p in range(pairs):
            at = (2 * p + i2) * samples
            piece = jnp.where(place == p, folded[at:at + samples], piece)
        pieces.append(piece)
    a_full = jnp.concatenate(pieces, axis=0)
    a = a_full.astype(BF16)
    a_t = a_full.T.astype(BF16)
    first = iota((1, lanes), 1) < total
    own_lanes = [
        jnp.where(
            first,
            jnp.broadcast_to(lf[2 * p:2 * p + 1, width:width + 1], (1, lanes)),
            jnp.broadcast_to(lf[2 * p + 1:2 * p + 2, width:width + 1], (1, lanes)),
        )
        for p in range(pairs)
    ]

    cot_copy.wait_recv()
    cot = cot_v[...].reshape(2 * rows * total, z)
    g_raw[...] = mm_nt(w_own, cot)

    copy(0, gat.at[pl.ds(0, n - 1)], gat.at[pl.ds(0, n - 1)], partner).wait_recv()
    ext = jnp.zeros((rows, lanes), F32)
    for p in range(n):
        ext = ext + gat[p, :, q:].astype(F32)
    gb_ref[...] = ext[0:1, :z] + ext[1:2, :z]
    inverse = [1.0 / (EPSILON + jnp.minimum(ext[2:3], own_lanes[p])) for p in range(pairs)]
    b = jnp.concatenate([gat[p, :, :q].astype(F32) for p in range(n)], axis=0)
    b_t[...] = jnp.concatenate([b, b], axis=0).T
    in_first = iota((samples, lanes), 1) < total
    for d in range(half):
        rows_d = jnp.concatenate(
            [b_t[h * part + d * LOW:h * part + (d + 1) * LOW] for h in range(highs)], axis=0
        )
        w_ref[:samples, d * lanes:(d + 1) * lanes] = jnp.where(in_first, rows_d, 0.0).astype(BF16)
        w_ref[samples:, d * lanes:(d + 1) * lanes] = jnp.where(in_first, 0.0, rows_d).astype(BF16)
    for d in range(0, half, 2):
        product = mm(a_t, w_ref[:, d * lanes:(d + 2) * lanes])
        for e in range(2):
            for p in range(pairs):
                o_ref[(d + e) * C:(d + e + 1) * C, p * lanes:(p + 1) * lanes] = (
                    product[p * C:(p + 1) * C, e * lanes:(e + 1) * lanes] * inverse[p]
                ).astype(BF16)
    gw = mm(o_ref[...], cot)
    gw = jnp.concatenate(
        [
            jnp.concatenate([gw[d * C + t * LOW:d * C + (t + 1) * LOW] for d in range(half)], axis=0)
            for t in range(tops)
        ],
        axis=1,
    )
    gw = mm(settle, gw.astype(BF16))
    for t in range(tops):
        send_w[t * part:(t + 1) * part] = gw[:, t * z:(t + 1) * z].astype(BF16)

    def chunk_of(m):
        return pl.ds(pl.multiple_of(m * chunk, chunk), chunk)

    alike(lambda p: copy(3, send_w.at[chunk_of(p // 2)], recv_w.at[chip], p).start())

    for d in range(half):
        for p in range(pairs):
            g_ref[p * C:(p + 1) * C, d * lanes:(d + 1) * lanes] = (
                g_raw[d * C:(d + 1) * C, p * lanes:(p + 1) * lanes] * inverse[p]
            ).astype(BF16)
    for d in range(0, half, 2):
        product = mm(a, g_ref[:, d * lanes:(d + 2) * lanes])
        for e in range(2):
            view = product[:, e * lanes:(e + 1) * lanes]
            chosen = jnp.where(in_first, view[:samples], view[samples:])
            for h in range(highs):
                r_t[h, (d + e) * LOW:(d + e + 1) * LOW] = chosen[h * LOW:(h + 1) * LOW]
    for h in range(highs):
        flat = r_t[h].T
        flat = (flat[:total] + flat[total:]).astype(BF16)
        for p in range(n):
            send_r[p, :, h * part:(h + 1) * part] = flat[p * rows:(p + 1) * rows]
    everyone(lambda p: copy(4, send_r.at[p], recv_r.at[me], p).start())
    recv_r[me] = send_r[me]

    left_sum = mm_nt(g_ref[...], w_ref[...])
    tall = rows * C // 2
    for k in range(2):
        gl_part[k] = left_sum[k * tall:(k + 1) * tall]
    gl_copy = copy(5, gl_part.at[1 - core], gl_got, partner)
    gl_copy.start()

    update = mm(w_t, o_ref[...])
    for p in range(pairs):
        flat = update[:, p * lanes:(p + 1) * lanes].T
        for e in range(2):
            i = 2 * p + e
            pu_part[i // rows, i % rows] = flat[e * total:(e + 1) * total]
    pu_copy = copy(6, pu_part.at[1 - core], pu_got, partner)
    pu_copy.start()

    own_chunk = send_w[chunk_of(chip)].astype(F32)
    all_recv = copy(3, send_w.at[pl.ds(0, (chips - 1) * chunk)], send_w.at[pl.ds(0, (chips - 1) * chunk)], partner)
    recv_w[chip] = jnp.zeros((chunk, z), BF16)
    all_recv.wait_recv()
    total_w = own_chunk
    for m in range(chips):
        total_w = total_w + recv_w[m].astype(F32)
    mine_w[...] = total_w.astype(BF16)

    def direct(p):
        return copy(7, mine_w, all_w.at[core, chip], p, ag_sems.at[chip])

    def landed(p):
        return copy(8, all_w.at[core, p // 2], all_w.at[core, p // 2], partner)

    alike(lambda p: direct(p).start())
    copy(8, mine_w, all_w.at[core, chip], partner).start()
    all_w[core, chip] = mine_w[...]

    gl_copy.wait_recv()
    owned = gl_part[core] + gl_got[...]
    owned = owned.T
    high, low = split(owned)
    unfold = one_hot(
        (iota((pairs * C // 2, pairs // 2 * block), 0) % C == iota((pairs * C // 2, pairs // 2 * block), 1) % C)
        & (iota((pairs * C // 2, pairs // 2 * block), 0) // C == iota((pairs * C // 2, pairs // 2 * block), 1) // block)
    )
    opened = mm(high, unfold) + mm(low, unfold)
    for p in range(pairs // 2):
        for i2 in range(2):
            for h in range(highs):
                at = i2 * samples + h * LOW
                view = opened[at:at + LOW, p * block:(p + 1) * block]
                gl_ref[2 * p + i2:2 * p + i2 + 1, h * block:(h + 1) * block] = jnp.sum(
                    jnp.where(diagonal, view, 0.0), axis=0, keepdims=True
                )
    gl_ref[...] = jnp.where(kept, gl_ref[...], 0.0)

    pu_copy.wait_recv()
    for i in range(rows):
        pu_ref[i] = (pu_part[core, i] + pu_got[i] + bias_v[...]).astype(BF16)

    copy(4, send_r.at[pl.ds(0, n - 1)], recv_r.at[pl.ds(0, n - 1)], partner).wait_recv()
    sums = []
    for k in range(2):
        acc = jnp.zeros((rows, q), F32)
        for m in range(chips):
            acc = acc + recv_r[2 * m + k].astype(F32)
        sums.append(acc)
    joined = jnp.concatenate(
        [
            jnp.concatenate([sums[k][:, h * part:(h + 1) * part] for k in range(2)], axis=1)
            for h in range(highs)
        ],
        axis=0,
    )
    high, low = split(joined)
    natural = mm_nt(high, perm) + mm_nt(low, perm)
    natural = jnp.concatenate([natural[h * rows:(h + 1) * rows] for h in range(highs)], axis=1)
    gr_ref[...] = jnp.where(kept, natural, 0.0)

    def forward(p):
        pltpu.make_async_remote_copy(
            src_ref=mine_w, dst_ref=all_w.at[core, p // 2],
            send_sem=send_sems.at[7], recv_sem=ag_sems.at[p // 2],
            device_id={"pi": partner}, device_id_type=MESH,
        ).wait_recv()
        landed(p).start()

    each(forward, 2, n, 2)
    copy(8, all_w.at[1 - core], all_w.at[1 - core], partner).wait_recv()
    gw_ref[...] = all_w[...]

    copy(0, gat.at[pl.ds(0, n - 1)], gat.at[pl.ds(0, n - 1)], partner).wait_send()
    left_copy.wait_send()
    cot_copy.wait_send()
    all_recv.wait_send()
    copy(4, send_r.at[pl.ds(0, n - 1)], recv_r.at[pl.ds(0, n - 1)], partner).wait_send()
    gl_copy.wait_send()
    pu_copy.wait_send()
    copy(7, send_w.at[pl.ds(0, (chips - 1) * chunk)], send_w.at[pl.ds(0, (chips - 1) * chunk)], partner).wait_send()
    copy(8, all_w.at[core], all_w.at[core], partner).wait_send()


def finish(pu, gl, gr, gw, gb, pu_out, gl_out, gr_out, gw_out, gb_out):
    pu_out[...] = pu[...]
    gl_out[...] = gl[...]
    gr_out[...] = gr[...]
    gb_out[...] = gb[...]
    half = C // 2
    for k in range(2):
        whole = gw[k].reshape(C * half, gw.shape[-1]).astype(F32)
        for c in range(C):
            gw_out[c * C + k * half:c * C + (k + 1) * half] = whole[c * half:(c + 1) * half]


def local(n, left, right, depth, w_out, bias, pair_cot):
    rows, width = left.shape
    total, z = pair_cot.shape[1:]
    chips = n // 2
    samples = width // C
    q = width // 2
    lanes = 2 * total
    size = C * C // 2
    chunk = size // chips
    limit = (24 if n <= 32 else 58) * 1024 * 1024
    vmem = pl.BlockSpec(memory_space=pltpu.VMEM)
    hbm = pl.BlockSpec(memory_space=pltpu.HBM)
    shapes = (
        jax.ShapeDtypeStruct((rows, total, z), BF16),
        jax.ShapeDtypeStruct((rows, width), F32),
        jax.ShapeDtypeStruct((rows, width), F32),
        jax.ShapeDtypeStruct((2, chips, chunk, z), BF16),
        jax.ShapeDtypeStruct((1, z), F32),
    )
    inputs = [
        pltpu.with_memory_space_constraint(v, pltpu.HBM)
        for v in (left, right, depth[None, :], pair_cot, w_out, bias[None, :])
    ]
    results = pl.pallas_call(
        functools.partial(kernel, n),
        out_shape=shapes,
        in_specs=[hbm] * 6,
        out_specs=(vmem,) * 5,
        scratch_shapes=[
            pltpu.VMEM((rows, width), BF16),
            pltpu.VMEM((rows, width), BF16),
            pltpu.VMEM((1, rows), jnp.int32),
            pltpu.VMEM((2, rows, total, z), BF16),
            pltpu.VMEM((C * C, z), BF16),
            pltpu.VMEM((1, z), F32),
            pltpu.VMEM((2, rows, q + lanes), BF16),
            pltpu.VMEM((n, rows, q + lanes), BF16),
            pltpu.VMEM((2, rows, width + z), BF16),
            pltpu.VMEM((2 * rows, width + z), F32),
            pltpu.VMEM((q, lanes), F32),
            pltpu.VMEM((2 * samples, C // 2 * lanes), BF16),
            pltpu.VMEM((size, rows * lanes), BF16),
            pltpu.VMEM((size, rows * lanes), F32),
            pltpu.VMEM((rows * C, C // 2 * lanes), BF16),
            pltpu.VMEM((size, z), BF16),
            pltpu.VMEM((1, chunk, z), F32),
            pltpu.VMEM((chips, chunk, z), BF16),
            pltpu.VMEM((chunk, z), BF16),
            pltpu.VMEM((2, chips, chunk, z), BF16),
            pltpu.VMEM((n, rows, q), BF16),
            pltpu.VMEM((n, rows, q), BF16),
            pltpu.VMEM((samples // LOW, C // 2 * LOW, lanes), F32),
            pltpu.VMEM((2, rows, total, z), F32),
            pltpu.VMEM((rows, total, z), F32),
            pltpu.VMEM((2, rows * C // 2, 2 * samples), F32),
            pltpu.VMEM((rows * C // 2, 2 * samples), F32),
            pltpu.SemaphoreType.DMA((6,)),
            pltpu.SemaphoreType.DMA((9,)),
            pltpu.SemaphoreType.DMA((9,)),
            pltpu.SemaphoreType.DMA((chips,)),
        ],
        compiler_params=pltpu.CompilerParams(collective_id=0, has_side_effects=True, vmem_limit_bytes=limit),
    )(*inputs)
    pu, gl, gr, gw, gb = pl.pallas_call(
        finish,
        out_shape=shapes[:3] + (jax.ShapeDtypeStruct((C * C, z), F32),) + shapes[4:],
        in_specs=[vmem] * 5,
        out_specs=(vmem,) * 5,
        compiler_params=pltpu.CompilerParams(vmem_limit_bytes=limit),
    )(*results)
    return pu, gl, gr, gw, gb.reshape(z)


def solution(mesh):
    placed = (
        P(("grp", "pi"), None),
        P(("grp", "pi"), None),
        P(("grp", "pi")),
        P(),
        P(),
        P(("grp", "pi"), None, None),
    )
    return jax.shard_map(
        functools.partial(local, mesh.shape["pi"]),
        mesh=mesh,
        in_specs=placed,
        out_specs=(
            P(("grp", "pi"), None, None),
            P(("grp", "pi"), None),
            P(("grp", "pi"), None),
            P("grp", None),
            P("grp"),
        ),
        check_vma=False,
    )
```

```python
import functools

import jax
import jax.numpy as jnp
from jax import lax
from jax.experimental import pallas as pl
from jax.experimental.pallas import tpu as pltpu
from jax.sharding import PartitionSpec as P

C = 32
LOW = 8
EPSILON = 0.001
MESH = pl.DeviceIdType.MESH
F32 = jnp.float32
BF16 = jnp.bfloat16
I32 = jnp.int32


def split(x):
    high = x.astype(BF16)
    return high, (x - high.astype(F32)).astype(BF16)


def mm(x, y):
    return jnp.dot(x, y, preferred_element_type=F32)


def mm_nt(x, y):
    return lax.dot_general(x, y, (((1,), (1,)), ((), ())), preferred_element_type=F32)


def iota(shape, axis):
    return lax.broadcasted_iota(I32, shape, axis)


def one_hot(hit):
    return hit.astype(F32).astype(BF16)


def kernel(
    n, left_in, right_in, depth_in, cot_in, w_in, bias_in,
    pu_ref, gl_ref, gr_ref, all_w, gb_ref, perm_ref,
    left_v, right_v, depth_v, cot_v, w_v, bias_v,
    xs, gat, xl, lf, b_t, w_ref, o_ref, g_raw, g_ref, send_w, recv_w, mine_w,
    send_r, recv_r, r_t, pu_part, pu_got, gl_part, gl_got,
    local_sems, send_sems, recv_sems, ag_sems,
):
    me = lax.axis_index("pi")
    rows, width = right_v.shape
    z = w_v.shape[1]
    samples = width // C
    total = cot_v.shape[2]
    chips = n // 2
    core = lax.rem(me, 2)
    chip = me // 2
    partner = me + 1 - 2 * core
    half = C // 2
    block = LOW * C
    highs = samples // LOW
    part = half * LOW
    q = highs * part
    pairs = rows
    lanes = 2 * total
    stages, span = mine_w.shape[:2]
    step = half // stages

    bits = [1 << k for k in range((n - 1).bit_length())]
    mine = [lax.rem(me // v, 2) for v in bits]

    def peer(x):
        where = 0
        for v, own in zip(bits, mine):
            where = where + v * lax.rem(own + (x // v) % 2, 2)
        return where

    def each(act, start, stop, step):
        if n <= 32:
            for x in range(start, stop, step):
                act(peer(x))
        else:
            def body(t, carry):
                act(peer(start + step * t))
                return carry

            lax.fori_loop(0, len(range(start, stop, step)), body, 0)

    def everyone(act):
        each(act, n - 1, 0, -1)

    def alike(act):
        each(act, n - 2, 0, -2)

    def copy(k, source, target, p, recv=None, k_send=None):
        return pltpu.make_async_remote_copy(
            src_ref=source, dst_ref=target,
            send_sem=send_sems.at[k if k_send is None else k_send], recv_sem=recv_sems.at[k] if recv is None else recv,
            device_id={"pi": p}, device_id_type=MESH,
        )

    def fetch(k, source, target):
        return pltpu.make_async_copy(source, target, local_sems.at[k])

    fetches = [
        fetch(0, right_in, right_v), fetch(1, depth_in, depth_v), fetch(2, cot_in, cot_v.at[core]),
        fetch(3, left_in, left_v), fetch(4, w_in, w_v), fetch(5, bias_in, bias_v),
    ]
    for f in fetches[:2]:
        f.start()
    barrier = pltpu.get_barrier_semaphore()
    everyone(
        lambda p: pl.semaphore_signal(barrier, inc=1, device_id={"pi": p}, device_id_type=MESH)
    )
    for f in fetches[2:]:
        f.start()

    perm = one_hot(
        (iota((block, block), 0) % C == iota((block, block), 1) // LOW)
        & (iota((block, block), 0) // C == iota((block, block), 1) % LOW)
    )
    fetches[0].wait()
    fetches[1].wait()
    spot = (rows, rows)
    wide = jnp.broadcast_to(depth_v[...], spot).astype(F32)
    own_depth = jnp.sum(
        jnp.where(iota(spot, 0) == iota(spot, 1), wide, 0.0), axis=1, keepdims=True
    )
    kept = (iota((rows, width), 1) // C).astype(F32) < jnp.broadcast_to(own_depth, (rows, width))
    right = jnp.where(kept, right_v[...].astype(F32), 0.0)
    stacked = jnp.concatenate([right[:, h * block:(h + 1) * block] for h in range(highs)], axis=0)
    moved = mm(stacked.astype(BF16), perm)
    perm_ref[...] = perm
    for k in range(2):
        for h in range(highs):
            xs[k, :, h * part:(h + 1) * part] = (
                moved[h * rows:(h + 1) * rows, k * part:(k + 1) * part].astype(BF16)
            )
    fetches[2].wait()
    cot_sum = jnp.zeros((1, z), F32)
    for i in range(rows):
        cot_sum = cot_sum + jnp.sum(cot_v[core, i].astype(F32), axis=0, keepdims=True)
    high, low = split(cot_sum)
    spread = jnp.where(
        iota((rows, lanes), 1) % total == me * rows + iota((rows, lanes), 0),
        jnp.broadcast_to(own_depth, (rows, lanes)), 0.0,
    )
    places = jnp.sum(spread, axis=0, keepdims=True)
    parts = [high.astype(F32), low.astype(F32)]
    if lanes > z:
        parts = [jnp.concatenate([v, jnp.zeros((1, lanes - z), F32)], axis=1) for v in parts]
    extra = jnp.concatenate(parts + [places, jnp.zeros((rows - 3, lanes), F32)], axis=0).astype(BF16)
    for k in range(2):
        xs[k, :, q:] = extra
    fetches[3].wait()
    xl[core, :, :width] = jnp.where(kept, left_v[...].astype(F32), 0.0).astype(BF16)
    xl[core, :, width:] = jnp.broadcast_to(own_depth, (rows, z)).astype(BF16)
    gat[me] = xs[core]

    pl.semaphore_wait(barrier, n - 1)
    everyone(lambda p: copy(0, xs.at[lax.rem(p, 2)], gat.at[me], p).start())
    left_copy = copy(1, xl.at[core], xl.at[core], partner)
    cot_copy = copy(2, cot_in, cot_v.at[core], partner)
    left_copy.start()
    cot_copy.start()

    fetches[4].wait()
    fetches[5].wait()
    turned = one_hot(
        (iota((part, block), 1) % C == iota((part, block), 0) // LOW + half * core)
        & (iota((part, block), 1) // C == iota((part, block), 0) % LOW)
    )
    tops = C // LOW
    moved_w = mm(turned, jnp.concatenate([w_v[t * block:(t + 1) * block] for t in range(tops)], axis=1))
    w_half = jnp.concatenate(
        [moved_w[d * LOW:(d + 1) * LOW, t * z:(t + 1) * z] for d in range(half) for t in range(tops)],
        axis=0,
    )
    w_own = w_half.astype(BF16)
    w_t = w_half.T.astype(BF16)

    left_copy.wait_recv()
    for k in range(2):
        lf[k * rows:(k + 1) * rows] = xl[k].astype(F32)
    diagonal = iota((LOW, block), 1) // C == iota((LOW, block), 0)
    lines = [
        jnp.where(
            diagonal, jnp.broadcast_to(lf[i:i + 1, h * block:(h + 1) * block], (LOW, block)), 0.0
        )
        for i in range(2 * rows) for h in range(highs)
    ]
    fold = one_hot(iota((block, pairs * C), 0) % C == iota((block, pairs * C), 1) % C)
    folded = mm(jnp.concatenate(lines, axis=0).astype(BF16), fold)
    place = iota((samples, pairs * C), 1) // C
    pieces = []
    for i2 in range(2):
        piece = jnp.zeros((samples, pairs * C), F32)
        for p in range(pairs):
            at = (2 * p + i2) * samples
            piece = jnp.where(place == p, folded[at:at + samples], piece)
        pieces.append(piece)
    a_full = jnp.concatenate(pieces, axis=0)
    a = a_full.astype(BF16)
    a_t = a_full.T.astype(BF16)
    first = iota((1, lanes), 1) < total
    own_lanes = [
        jnp.where(
            first,
            jnp.broadcast_to(lf[2 * p:2 * p + 1, width:width + 1], (1, lanes)),
            jnp.broadcast_to(lf[2 * p + 1:2 * p + 2, width:width + 1], (1, lanes)),
        )
        for p in range(pairs)
    ]

    cot_copy.wait_recv()
    cot = cot_v[...].reshape(2 * rows * total, z)
    g_raw[...] = mm_nt(w_own, cot)

    copy(0, gat.at[pl.ds(0, n - 1)], gat.at[pl.ds(0, n - 1)], partner).wait_recv()
    ext = jnp.zeros((rows, lanes), F32)
    for p in range(n):
        ext = ext + gat[p, :, q:].astype(F32)
    gb_ref[...] = ext[0:1, :z] + ext[1:2, :z]
    inverse = [1.0 / (EPSILON + jnp.minimum(ext[2:3], own_lanes[p])) for p in range(pairs)]
    b = jnp.concatenate([gat[p, :, :q].astype(F32) for p in range(n)], axis=0)
    b_t[...] = jnp.concatenate([b, b], axis=0).T
    in_first = iota((samples, lanes), 1) < total
    for h in range(stages):
        for d in range(h * step, (h + 1) * step):
            rows_d = jnp.concatenate(
                [b_t[t * part + d * LOW:t * part + (d + 1) * LOW] for t in range(highs)], axis=0
            )
            w_ref[:samples, d * lanes:(d + 1) * lanes] = jnp.where(in_first, rows_d, 0.0).astype(BF16)
            w_ref[samples:, d * lanes:(d + 1) * lanes] = jnp.where(in_first, 0.0, rows_d).astype(BF16)
        for d in range(h * step, (h + 1) * step, 2):
            product = mm(a_t, w_ref[:, d * lanes:(d + 2) * lanes])
            for e in range(2):
                for p in range(pairs):
                    o_ref[(d + e) * C:(d + e + 1) * C, p * lanes:(p + 1) * lanes] = (
                        product[p * C:(p + 1) * C, e * lanes:(e + 1) * lanes] * inverse[p]
                    ).astype(BF16)
        gw = mm(o_ref[h * step * C:(h + 1) * step * C], cot).astype(BF16)
        for m in range(chips):
            send_w[h, m] = gw[m * span:(m + 1) * span]
        alike(lambda p: copy(3 + h, send_w.at[h, p // 2], recv_w.at[h, chip], p, k_send=3).start())

    for d in range(half):
        for p in range(pairs):
            g_ref[p * C:(p + 1) * C, d * lanes:(d + 1) * lanes] = (
                g_raw[d * C:(d + 1) * C, p * lanes:(p + 1) * lanes] * inverse[p]
            ).astype(BF16)
    for d in range(0, half, 2):
        product = mm(a, g_ref[:, d * lanes:(d + 2) * lanes])
        for e in range(2):
            view = product[:, e * lanes:(e + 1) * lanes]
            chosen = jnp.where(in_first, view[:samples], view[samples:])
            for h in range(highs):
                r_t[h, (d + e) * LOW:(d + e + 1) * LOW] = chosen[h * LOW:(h + 1) * LOW]
    for h in range(highs):
        flat = r_t[h].T
        flat = (flat[:total] + flat[total:]).astype(BF16)
        for p in range(n):
            send_r[p, :, h * part:(h + 1) * part] = flat[p * rows:(p + 1) * rows]
    recv_r[me] = send_r[me]

    left_sum = mm_nt(g_ref[...], w_ref[...])
    tall = rows * C // 2
    for k in range(2):
        gl_part[k] = left_sum[k * tall:(k + 1) * tall]
    gl_copy = copy(6, gl_part.at[1 - core], gl_got, partner)
    gl_copy.start()

    update = mm(w_t, o_ref[...])
    for p in range(pairs):
        flat = update[:, p * lanes:(p + 1) * lanes].T
        for e in range(2):
            i = 2 * p + e
            pu_part[i // rows, i % rows] = flat[e * total:(e + 1) * total]
    pu_copy = copy(7, pu_part.at[1 - core], pu_got, partner)
    pu_copy.start()

    def direct(h, p):
        return copy(8, mine_w.at[h], all_w.at[core, h, chip], p, ag_sems.at[h, chip])

    def arrived(h, p):
        return copy(8, mine_w.at[h], all_w.at[core, h, p // 2], partner, ag_sems.at[h, p // 2])

    def landed(h, p):
        return copy(9, all_w.at[core, h, p // 2], all_w.at[core, h, p // 2], partner)

    for h in range(stages):
        recv_w[h, chip] = send_w[h, chip]
    for h in range(stages):
        copy(
            3 + h, send_w.at[h, pl.ds(0, chips - 1)], recv_w.at[h, pl.ds(0, chips - 1)], partner, k_send=3
        ).wait_recv()
        if h == 0:
            everyone(lambda p: copy(5, send_r.at[p], recv_r.at[me], p).start())
        total_w = jnp.zeros((span, z), F32)
        for m in range(chips):
            total_w = total_w + recv_w[h, m].astype(F32)
        mine_w[h] = total_w.astype(BF16)
        alike(lambda p: direct(h, p).start())
        copy(9, mine_w.at[h], all_w.at[core, h, chip], partner).start()
        all_w[core, h, chip] = mine_w[h]

    gl_copy.wait_recv()
    owned = gl_part[core] + gl_got[...]
    owned = owned.T
    high, low = split(owned)
    unfold = one_hot(
        (iota((pairs * C // 2, pairs // 2 * block), 0) % C == iota((pairs * C // 2, pairs // 2 * block), 1) % C)
        & (iota((pairs * C // 2, pairs // 2 * block), 0) // C == iota((pairs * C // 2, pairs // 2 * block), 1) // block)
    )
    opened = mm(high, unfold) + mm(low, unfold)
    for p in range(pairs // 2):
        for i2 in range(2):
            for h in range(highs):
                at = i2 * samples + h * LOW
                view = opened[at:at + LOW, p * block:(p + 1) * block]
                gl_ref[2 * p + i2:2 * p + i2 + 1, h * block:(h + 1) * block] = jnp.sum(
                    jnp.where(diagonal, view, 0.0), axis=0, keepdims=True
                )
    gl_ref[...] = jnp.where(kept, gl_ref[...], 0.0)

    pu_copy.wait_recv()
    for i in range(rows):
        pu_ref[i] = (pu_part[core, i] + pu_got[i] + bias_v[...]).astype(BF16)

    copy(5, send_r.at[pl.ds(0, n - 1)], recv_r.at[pl.ds(0, n - 1)], partner).wait_recv()
    sums = []
    for k in range(2):
        acc = jnp.zeros((rows, q), F32)
        for m in range(chips):
            acc = acc + recv_r[2 * m + k].astype(F32)
        sums.append(acc)
    joined = jnp.concatenate(
        [
            jnp.concatenate([sums[k][:, h * part:(h + 1) * part] for k in range(2)], axis=1)
            for h in range(highs)
        ],
        axis=0,
    )
    high, low = split(joined)
    natural = mm_nt(high, perm) + mm_nt(low, perm)
    natural = jnp.concatenate([natural[h * rows:(h + 1) * rows] for h in range(highs)], axis=1)
    gr_ref[...] = jnp.where(kept, natural, 0.0)

    for h in range(stages):
        def forward(p):
            arrived(h, p).wait_recv()
            landed(h, p).start()

        each(forward, 2, n, 2)
    copy(9, all_w.at[1 - core], all_w.at[1 - core], partner).wait_recv()

    copy(0, gat.at[pl.ds(0, n - 1)], gat.at[pl.ds(0, n - 1)], partner).wait_send()
    left_copy.wait_send()
    cot_copy.wait_send()
    copy(3, send_w.at[:, pl.ds(0, chips - 1)], send_w.at[:, pl.ds(0, chips - 1)], partner).wait_send()
    copy(5, send_r.at[pl.ds(0, n - 1)], recv_r.at[pl.ds(0, n - 1)], partner).wait_send()
    gl_copy.wait_send()
    pu_copy.wait_send()
    copy(8, send_w.at[:, pl.ds(0, chips - 1)], send_w.at[:, pl.ds(0, chips - 1)], partner).wait_send()
    copy(9, all_w.at[core], all_w.at[core], partner).wait_send()


def finish(pu, gl, gr, gw, gb, perm, pu_out, gl_out, gr_out, gw_out, gb_out):
    pu_out[...] = pu[...]
    gl_out[...] = gl[...]
    gr_out[...] = gr[...]
    gb_out[...] = gb[...]
    z = gw.shape[-1]
    block = LOW * C
    whole = gw[...].reshape(C * C, z).astype(F32)
    sides = [
        jnp.concatenate(
            [whole[d * C + t * LOW:d * C + (t + 1) * LOW] for d in range(C)], axis=0
        ).astype(BF16)
        for t in range(C // LOW)
    ]
    for t in range(0, C // LOW, 2):
        moved = mm(perm[...], jnp.concatenate(sides[t:t + 2], axis=1))
        for e in range(2):
            gw_out[(t + e) * block:(t + e + 1) * block] = moved[:, e * z:(e + 1) * z]


def local(n, left, right, depth, w_out, bias, pair_cot):
    rows, width = left.shape
    total, z = pair_cot.shape[1:]
    chips = n // 2
    samples = width // C
    q = width // 2
    lanes = 2 * total
    size = C * C // 2
    stages = 2 if size // chips % 16 == 0 else 1
    piece = size // chips // stages
    block = LOW * C
    limit = (24 if n <= 32 else 58) * 1024 * 1024
    vmem = pl.BlockSpec(memory_space=pltpu.VMEM)
    hbm = pl.BlockSpec(memory_space=pltpu.HBM)
    shapes = (
        jax.ShapeDtypeStruct((rows, total, z), BF16),
        jax.ShapeDtypeStruct((rows, width), F32),
        jax.ShapeDtypeStruct((rows, width), F32),
        jax.ShapeDtypeStruct((2, stages, chips, piece, z), BF16),
        jax.ShapeDtypeStruct((1, z), F32),
        jax.ShapeDtypeStruct((block, block), BF16),
    )
    inputs = [
        pltpu.with_memory_space_constraint(v, pltpu.HBM)
        for v in (left, right, depth[None, :], pair_cot, w_out, bias[None, :])
    ]
    results = pl.pallas_call(
        functools.partial(kernel, n),
        out_shape=shapes,
        in_specs=[hbm] * 6,
        out_specs=(vmem,) * 6,
        scratch_shapes=[
            pltpu.VMEM((rows, width), BF16),
            pltpu.VMEM((rows, width), BF16),
            pltpu.VMEM((1, rows), jnp.int32),
            pltpu.VMEM((2, rows, total, z), BF16),
            pltpu.VMEM((C * C, z), BF16),
            pltpu.VMEM((1, z), F32),
            pltpu.VMEM((2, rows, q + lanes), BF16),
            pltpu.VMEM((n, rows, q + lanes), BF16),
            pltpu.VMEM((2, rows, width + z), BF16),
            pltpu.VMEM((2 * rows, width + z), F32),
            pltpu.VMEM((q, lanes), F32),
            pltpu.VMEM((2 * samples, C // 2 * lanes), BF16),
            pltpu.VMEM((size, rows * lanes), BF16),
            pltpu.VMEM((size, rows * lanes), F32),
            pltpu.VMEM((rows * C, C // 2 * lanes), BF16),
            pltpu.VMEM((stages, chips, piece, z), BF16),
            pltpu.VMEM((stages, chips, piece, z), BF16),
            pltpu.VMEM((stages, piece, z), BF16),
            pltpu.VMEM((n, rows, q), BF16),
            pltpu.VMEM((n, rows, q), BF16),
            pltpu.VMEM((samples // LOW, C // 2 * LOW, lanes), F32),
            pltpu.VMEM((2, rows, total, z), F32),
            pltpu.VMEM((rows, total, z), F32),
            pltpu.VMEM((2, rows * C // 2, 2 * samples), F32),
            pltpu.VMEM((rows * C // 2, 2 * samples), F32),
            pltpu.SemaphoreType.DMA((6,)),
            pltpu.SemaphoreType.DMA((10,)),
            pltpu.SemaphoreType.DMA((10,)),
            pltpu.SemaphoreType.DMA((stages, chips)),
        ],
        compiler_params=pltpu.CompilerParams(collective_id=0, has_side_effects=True, vmem_limit_bytes=limit),
    )(*inputs)
    pu, gl, gr, gw, gb = pl.pallas_call(
        finish,
        out_shape=shapes[:3] + (jax.ShapeDtypeStruct((C * C, z), F32),) + shapes[4:5],
        in_specs=[vmem] * 6,
        out_specs=(vmem,) * 5,
        compiler_params=pltpu.CompilerParams(vmem_limit_bytes=limit),
    )(*results)
    return pu, gl, gr, gw, gb.reshape(z)


def solution(mesh):
    placed = (
        P(("grp", "pi"), None),
        P(("grp", "pi"), None),
        P(("grp", "pi")),
        P(),
        P(),
        P(("grp", "pi"), None, None),
    )
    return jax.shard_map(
        functools.partial(local, mesh.shape["pi"]),
        mesh=mesh,
        in_specs=placed,
        out_specs=(
            P(("grp", "pi"), None, None),
            P(("grp", "pi"), None),
            P(("grp", "pi"), None),
            P("grp", None),
            P("grp"),
        ),
        check_vma=False,
    )
```

```python
import functools

import jax
import jax.numpy as jnp
from jax import lax
from jax.experimental import pallas as pl
from jax.experimental.pallas import tpu as pltpu
from jax.sharding import PartitionSpec as P

C = 32
LOW = 8
EPSILON = 0.001
MESH = pl.DeviceIdType.MESH
F32 = jnp.float32
BF16 = jnp.bfloat16
I32 = jnp.int32


def split(x):
    high = x.astype(BF16)
    return high, (x - high.astype(F32)).astype(BF16)


def mm(x, y):
    return jnp.dot(x, y, preferred_element_type=F32)


def mm_nt(x, y):
    return lax.dot_general(x, y, (((1,), (1,)), ((), ())), preferred_element_type=F32)


def iota(shape, axis):
    return lax.broadcasted_iota(I32, shape, axis)


def one_hot(hit):
    return hit.astype(F32).astype(BF16)


def kernel(
    n, left_in, right_in, depth_in, cot_in, w_in, bias_in,
    pu_ref, gl_ref, gr_ref, all_w, gb_ref, perm_ref,
    left_v, right_v, depth_v, cot_v, w_v, bias_v,
    xs, gat, xl, lf, b_t, w_ref, o_ref, g_raw, g_ref, send_w, recv_w, mine_w,
    send_r, recv_r, r_t, pu_part, pu_got, gl_part, gl_got,
    local_sems, send_sems, recv_sems, ag_sems,
):
    me = lax.axis_index("pi")
    rows, width = right_v.shape
    z = w_v.shape[1]
    samples = width // C
    total = cot_v.shape[2]
    chips = n // 2
    core = lax.rem(me, 2)
    chip = me // 2
    partner = me + 1 - 2 * core
    half = C // 2
    block = LOW * C
    highs = samples // LOW
    part = half * LOW
    q = highs * part
    pairs = rows
    lanes = 2 * total
    stages, span = mine_w.shape[:2]
    step = half // stages

    bits = [1 << k for k in range((n - 1).bit_length())]
    mine = [lax.rem(me // v, 2) for v in bits]

    def peer(x):
        where = 0
        for v, own in zip(bits, mine):
            where = where + v * lax.rem(own + (x // v) % 2, 2)
        return where

    def each(act, start, stop, step):
        if n <= 32:
            for x in range(start, stop, step):
                act(peer(x))
        else:
            def body(t, carry):
                act(peer(start + step * t))
                return carry

            lax.fori_loop(0, len(range(start, stop, step)), body, 0)

    def everyone(act):
        each(act, n - 1, 0, -1)

    def alike(act):
        each(act, n - 2, 0, -2)

    def copy(k, source, target, p, recv=None, k_send=None):
        return pltpu.make_async_remote_copy(
            src_ref=source, dst_ref=target,
            send_sem=send_sems.at[k if k_send is None else k_send], recv_sem=recv_sems.at[k] if recv is None else recv,
            device_id={"pi": p}, device_id_type=MESH,
        )

    def fetch(k, source, target):
        return pltpu.make_async_copy(source, target, local_sems.at[k])

    fetches = [
        fetch(0, right_in, right_v), fetch(1, depth_in, depth_v), fetch(2, cot_in, cot_v.at[core]),
        fetch(3, left_in, left_v), fetch(4, w_in, w_v), fetch(5, bias_in, bias_v),
    ]
    for f in fetches[:2]:
        f.start()
    barrier = pltpu.get_barrier_semaphore()
    everyone(
        lambda p: pl.semaphore_signal(barrier, inc=1, device_id={"pi": p}, device_id_type=MESH)
    )
    for f in fetches[2:]:
        f.start()

    perm = one_hot(
        (iota((block, block), 0) % C == iota((block, block), 1) // LOW)
        & (iota((block, block), 0) // C == iota((block, block), 1) % LOW)
    )
    fetches[0].wait()
    fetches[1].wait()
    spot = (rows, rows)
    wide = jnp.broadcast_to(depth_v[...], spot).astype(F32)
    own_depth = jnp.sum(
        jnp.where(iota(spot, 0) == iota(spot, 1), wide, 0.0), axis=1, keepdims=True
    )
    kept = (iota((rows, width), 1) // C).astype(F32) < jnp.broadcast_to(own_depth, (rows, width))
    right = jnp.where(kept, right_v[...].astype(F32), 0.0)
    stacked = jnp.concatenate([right[:, h * block:(h + 1) * block] for h in range(highs)], axis=0)
    moved = mm(stacked.astype(BF16), perm)
    perm_ref[...] = perm
    for k in range(2):
        for h in range(highs):
            xs[k, :, h * part:(h + 1) * part] = (
                moved[h * rows:(h + 1) * rows, k * part:(k + 1) * part].astype(BF16)
            )
    fetches[2].wait()
    cot_sum = jnp.zeros((1, z), F32)
    for i in range(rows):
        cot_sum = cot_sum + jnp.sum(cot_v[core, i].astype(F32), axis=0, keepdims=True)
    high, low = split(cot_sum)
    spread = jnp.where(
        iota((rows, lanes), 1) % total == me * rows + iota((rows, lanes), 0),
        jnp.broadcast_to(own_depth, (rows, lanes)), 0.0,
    )
    places = jnp.sum(spread, axis=0, keepdims=True)
    parts = [high.astype(F32), low.astype(F32)]
    if lanes > z:
        parts = [jnp.concatenate([v, jnp.zeros((1, lanes - z), F32)], axis=1) for v in parts]
    extra = jnp.concatenate(parts + [places, jnp.zeros((rows - 3, lanes), F32)], axis=0).astype(BF16)
    for k in range(2):
        xs[k, :, q:] = extra
    fetches[3].wait()
    xl[core, :, :width] = jnp.where(kept, left_v[...].astype(F32), 0.0).astype(BF16)
    xl[core, :, width:] = jnp.broadcast_to(own_depth, (rows, z)).astype(BF16)
    gat[me] = xs[core]

    pl.semaphore_wait(barrier, n - 1)
    everyone(lambda p: copy(0, xs.at[lax.rem(p, 2)], gat.at[me], p).start())
    left_copy = copy(1, xl.at[core], xl.at[core], partner)
    cot_copy = copy(2, cot_in, cot_v.at[core], partner)
    left_copy.start()
    cot_copy.start()

    fetches[4].wait()
    fetches[5].wait()
    turned = one_hot(
        (iota((part, block), 1) % C == iota((part, block), 0) // LOW + half * core)
        & (iota((part, block), 1) // C == iota((part, block), 0) % LOW)
    )
    tops = C // LOW
    moved_w = mm(turned, jnp.concatenate([w_v[t * block:(t + 1) * block] for t in range(tops)], axis=1))
    w_half = jnp.concatenate(
        [moved_w[d * LOW:(d + 1) * LOW, t * z:(t + 1) * z] for d in range(half) for t in range(tops)],
        axis=0,
    )
    w_own = w_half.astype(BF16)
    w_t = w_half.T.astype(BF16)

    left_copy.wait_recv()
    for k in range(2):
        lf[k * rows:(k + 1) * rows] = xl[k].astype(F32)
    diagonal = iota((LOW, block), 1) // C == iota((LOW, block), 0)
    lines = [
        jnp.where(
            diagonal, jnp.broadcast_to(lf[i:i + 1, h * block:(h + 1) * block], (LOW, block)), 0.0
        )
        for i in range(2 * rows) for h in range(highs)
    ]
    fold = one_hot(iota((block, pairs * C), 0) % C == iota((block, pairs * C), 1) % C)
    folded = mm(jnp.concatenate(lines, axis=0).astype(BF16), fold)
    place = iota((samples, pairs * C), 1) // C
    pieces = []
    for i2 in range(2):
        piece = jnp.zeros((samples, pairs * C), F32)
        for p in range(pairs):
            at = (2 * p + i2) * samples
            piece = jnp.where(place == p, folded[at:at + samples], piece)
        pieces.append(piece)
    a_full = jnp.concatenate(pieces, axis=0)
    a = a_full.astype(BF16)
    a_t = a_full.T.astype(BF16)
    first = iota((1, lanes), 1) < total
    own_lanes = [
        jnp.where(
            first,
            jnp.broadcast_to(lf[2 * p:2 * p + 1, width:width + 1], (1, lanes)),
            jnp.broadcast_to(lf[2 * p + 1:2 * p + 2, width:width + 1], (1, lanes)),
        )
        for p in range(pairs)
    ]

    cot_copy.wait_recv()
    cot = cot_v[...].reshape(2 * rows * total, z)
    g_raw[...] = mm_nt(w_own, cot)

    copy(0, gat.at[pl.ds(0, n - 1)], gat.at[pl.ds(0, n - 1)], partner).wait_recv()
    ext = jnp.zeros((rows, lanes), F32)
    for p in range(n):
        ext = ext + gat[p, :, q:].astype(F32)
    gb_ref[...] = ext[0:1, :z] + ext[1:2, :z]
    inverse = [1.0 / (EPSILON + jnp.minimum(ext[2:3], own_lanes[p])) for p in range(pairs)]
    b = jnp.concatenate([gat[p, :, :q].astype(F32) for p in range(n)], axis=0)
    b_t[...] = jnp.concatenate([b, b], axis=0).T
    in_first = iota((samples, lanes), 1) < total
    for h in range(stages):
        for d in range(h * step, (h + 1) * step):
            rows_d = jnp.concatenate(
                [b_t[t * part + d * LOW:t * part + (d + 1) * LOW] for t in range(highs)], axis=0
            )
            w_ref[:samples, d * lanes:(d + 1) * lanes] = jnp.where(in_first, rows_d, 0.0).astype(BF16)
            w_ref[samples:, d * lanes:(d + 1) * lanes] = jnp.where(in_first, 0.0, rows_d).astype(BF16)
        for d in range(h * step, (h + 1) * step, 2):
            product = mm(a_t, w_ref[:, d * lanes:(d + 2) * lanes])
            for e in range(2):
                for p in range(pairs):
                    o_ref[(d + e) * C:(d + e + 1) * C, p * lanes:(p + 1) * lanes] = (
                        product[p * C:(p + 1) * C, e * lanes:(e + 1) * lanes] * inverse[p]
                    ).astype(BF16)
        gw = mm(o_ref[h * step * C:(h + 1) * step * C], cot).astype(BF16)
        for m in range(chips):
            send_w[h, m] = gw[m * span:(m + 1) * span]
        alike(lambda p: copy(3 + h, send_w.at[h, p // 2], recv_w.at[h, chip], p, k_send=3).start())

    for d in range(half):
        for p in range(pairs):
            g_ref[p * C:(p + 1) * C, d * lanes:(d + 1) * lanes] = (
                g_raw[d * C:(d + 1) * C, p * lanes:(p + 1) * lanes] * inverse[p]
            ).astype(BF16)
    for d in range(0, half, 2):
        product = mm(a, g_ref[:, d * lanes:(d + 2) * lanes])
        for e in range(2):
            view = product[:, e * lanes:(e + 1) * lanes]
            chosen = jnp.where(in_first, view[:samples], view[samples:])
            for h in range(highs):
                r_t[h, (d + e) * LOW:(d + e + 1) * LOW] = chosen[h * LOW:(h + 1) * LOW]
    for h in range(highs):
        flat = r_t[h].T
        flat = (flat[:total] + flat[total:]).astype(BF16)
        for p in range(n):
            send_r[p, :, h * part:(h + 1) * part] = flat[p * rows:(p + 1) * rows]
    recv_r[me] = send_r[me]

    left_sum = mm_nt(g_ref[...], w_ref[...])
    tall = rows * C // 2
    for k in range(2):
        gl_part[k] = left_sum[k * tall:(k + 1) * tall]
    gl_copy = copy(6, gl_part.at[1 - core], gl_got, partner)
    gl_copy.start()

    update = mm(w_t, o_ref[...])
    for p in range(pairs):
        flat = update[:, p * lanes:(p + 1) * lanes].T
        for e in range(2):
            i = 2 * p + e
            pu_part[i // rows, i % rows] = flat[e * total:(e + 1) * total]
    pu_copy = copy(7, pu_part.at[1 - core], pu_got, partner)
    pu_copy.start()

    def direct(h, p):
        return copy(8, mine_w.at[h], all_w.at[core, h, chip], p, ag_sems.at[h, chip])

    def arrived(h, p):
        return copy(8, mine_w.at[h], all_w.at[core, h, p // 2], partner, ag_sems.at[h, p // 2])

    def landed(h, p):
        return copy(9, all_w.at[core, h, p // 2], all_w.at[core, h, p // 2], partner)

    for h in range(stages):
        recv_w[h, chip] = send_w[h, chip]
    for h in range(stages):
        copy(
            3 + h, send_w.at[h, pl.ds(0, chips - 1)], recv_w.at[h, pl.ds(0, chips - 1)], partner, k_send=3
        ).wait_recv()
        total_w = jnp.zeros((span, z), F32)
        for m in range(chips):
            total_w = total_w + recv_w[h, m].astype(F32)
        mine_w[h] = total_w.astype(BF16)
        alike(lambda p: direct(h, p).start())
        copy(9, mine_w.at[h], all_w.at[core, h, chip], partner).start()
        all_w[core, h, chip] = mine_w[h]

    everyone(lambda p: copy(5, send_r.at[p], recv_r.at[me], p).start())
    gl_copy.wait_recv()
    owned = gl_part[core] + gl_got[...]
    owned = owned.T
    high, low = split(owned)
    unfold = one_hot(
        (iota((pairs * C // 2, pairs // 2 * block), 0) % C == iota((pairs * C // 2, pairs // 2 * block), 1) % C)
        & (iota((pairs * C // 2, pairs // 2 * block), 0) // C == iota((pairs * C // 2, pairs // 2 * block), 1) // block)
    )
    opened = mm(high, unfold) + mm(low, unfold)
    for p in range(pairs // 2):
        for i2 in range(2):
            for h in range(highs):
                at = i2 * samples + h * LOW
                view = opened[at:at + LOW, p * block:(p + 1) * block]
                gl_ref[2 * p + i2:2 * p + i2 + 1, h * block:(h + 1) * block] = jnp.sum(
                    jnp.where(diagonal, view, 0.0), axis=0, keepdims=True
                )
    gl_ref[...] = jnp.where(kept, gl_ref[...], 0.0)

    pu_copy.wait_recv()
    for i in range(rows):
        pu_ref[i] = (pu_part[core, i] + pu_got[i] + bias_v[...]).astype(BF16)

    for h in range(stages):
        def forward(p):
            arrived(h, p).wait_recv()
            landed(h, p).start()

        each(forward, 2, n, 2)
    copy(5, send_r.at[pl.ds(0, n - 1)], recv_r.at[pl.ds(0, n - 1)], partner).wait_recv()
    sums = []
    for k in range(2):
        acc = jnp.zeros((rows, q), F32)
        for m in range(chips):
            acc = acc + recv_r[2 * m + k].astype(F32)
        sums.append(acc)
    joined = jnp.concatenate(
        [
            jnp.concatenate([sums[k][:, h * part:(h + 1) * part] for k in range(2)], axis=1)
            for h in range(highs)
        ],
        axis=0,
    )
    high, low = split(joined)
    natural = mm_nt(high, perm) + mm_nt(low, perm)
    natural = jnp.concatenate([natural[h * rows:(h + 1) * rows] for h in range(highs)], axis=1)
    gr_ref[...] = jnp.where(kept, natural, 0.0)

    copy(9, all_w.at[1 - core], all_w.at[1 - core], partner).wait_recv()

    copy(0, gat.at[pl.ds(0, n - 1)], gat.at[pl.ds(0, n - 1)], partner).wait_send()
    left_copy.wait_send()
    cot_copy.wait_send()
    copy(3, send_w.at[:, pl.ds(0, chips - 1)], send_w.at[:, pl.ds(0, chips - 1)], partner).wait_send()
    copy(5, send_r.at[pl.ds(0, n - 1)], recv_r.at[pl.ds(0, n - 1)], partner).wait_send()
    gl_copy.wait_send()
    pu_copy.wait_send()
    copy(8, send_w.at[:, pl.ds(0, chips - 1)], send_w.at[:, pl.ds(0, chips - 1)], partner).wait_send()
    copy(9, all_w.at[core], all_w.at[core], partner).wait_send()


def finish(pu, gl, gr, gw, gb, perm, pu_out, gl_out, gr_out, gw_out, gb_out):
    pu_out[...] = pu[...]
    gl_out[...] = gl[...]
    gr_out[...] = gr[...]
    gb_out[...] = gb[...]
    z = gw.shape[-1]
    block = LOW * C
    whole = gw[...].reshape(C * C, z).astype(F32)
    sides = [
        jnp.concatenate(
            [whole[d * C + t * LOW:d * C + (t + 1) * LOW] for d in range(C)], axis=0
        ).astype(BF16)
        for t in range(C // LOW)
    ]
    for t in range(0, C // LOW, 2):
        moved = mm(perm[...], jnp.concatenate(sides[t:t + 2], axis=1))
        for e in range(2):
            gw_out[(t + e) * block:(t + e + 1) * block] = moved[:, e * z:(e + 1) * z]


def local(n, left, right, depth, w_out, bias, pair_cot):
    rows, width = left.shape
    total, z = pair_cot.shape[1:]
    chips = n // 2
    samples = width // C
    q = width // 2
    lanes = 2 * total
    size = C * C // 2
    stages = 2 if size // chips % 16 == 0 else 1
    piece = size // chips // stages
    block = LOW * C
    limit = (24 if n <= 32 else 58) * 1024 * 1024
    vmem = pl.BlockSpec(memory_space=pltpu.VMEM)
    hbm = pl.BlockSpec(memory_space=pltpu.HBM)
    shapes = (
        jax.ShapeDtypeStruct((rows, total, z), BF16),
        jax.ShapeDtypeStruct((rows, width), F32),
        jax.ShapeDtypeStruct((rows, width), F32),
        jax.ShapeDtypeStruct((2, stages, chips, piece, z), BF16),
        jax.ShapeDtypeStruct((1, z), F32),
        jax.ShapeDtypeStruct((block, block), BF16),
    )
    inputs = [
        pltpu.with_memory_space_constraint(v, pltpu.HBM)
        for v in (left, right, depth[None, :], pair_cot, w_out, bias[None, :])
    ]
    results = pl.pallas_call(
        functools.partial(kernel, n),
        out_shape=shapes,
        in_specs=[hbm] * 6,
        out_specs=(vmem,) * 6,
        scratch_shapes=[
            pltpu.VMEM((rows, width), BF16),
            pltpu.VMEM((rows, width), BF16),
            pltpu.VMEM((1, rows), jnp.int32),
            pltpu.VMEM((2, rows, total, z), BF16),
            pltpu.VMEM((C * C, z), BF16),
            pltpu.VMEM((1, z), F32),
            pltpu.VMEM((2, rows, q + lanes), BF16),
            pltpu.VMEM((n, rows, q + lanes), BF16),
            pltpu.VMEM((2, rows, width + z), BF16),
            pltpu.VMEM((2 * rows, width + z), F32),
            pltpu.VMEM((q, lanes), F32),
            pltpu.VMEM((2 * samples, C // 2 * lanes), BF16),
            pltpu.VMEM((size, rows * lanes), BF16),
            pltpu.VMEM((size, rows * lanes), F32),
            pltpu.VMEM((rows * C, C // 2 * lanes), BF16),
            pltpu.VMEM((stages, chips, piece, z), BF16),
            pltpu.VMEM((stages, chips, piece, z), BF16),
            pltpu.VMEM((stages, piece, z), BF16),
            pltpu.VMEM((n, rows, q), BF16),
            pltpu.VMEM((n, rows, q), BF16),
            pltpu.VMEM((samples // LOW, C // 2 * LOW, lanes), F32),
            pltpu.VMEM((2, rows, total, z), F32),
            pltpu.VMEM((rows, total, z), F32),
            pltpu.VMEM((2, rows * C // 2, 2 * samples), F32),
            pltpu.VMEM((rows * C // 2, 2 * samples), F32),
            pltpu.SemaphoreType.DMA((6,)),
            pltpu.SemaphoreType.DMA((10,)),
            pltpu.SemaphoreType.DMA((10,)),
            pltpu.SemaphoreType.DMA((stages, chips)),
        ],
        compiler_params=pltpu.CompilerParams(collective_id=0, has_side_effects=True, vmem_limit_bytes=limit),
    )(*inputs)
    pu, gl, gr, gw, gb = pl.pallas_call(
        finish,
        out_shape=shapes[:3] + (jax.ShapeDtypeStruct((C * C, z), F32),) + shapes[4:5],
        in_specs=[vmem] * 6,
        out_specs=(vmem,) * 5,
        compiler_params=pltpu.CompilerParams(vmem_limit_bytes=limit),
    )(*results)
    return pu, gl, gr, gw, gb.reshape(z)


def solution(mesh):
    placed = (
        P(("grp", "pi"), None),
        P(("grp", "pi"), None),
        P(("grp", "pi")),
        P(),
        P(),
        P(("grp", "pi"), None, None),
    )
    return jax.shard_map(
        functools.partial(local, mesh.shape["pi"]),
        mesh=mesh,
        in_specs=placed,
        out_specs=(
            P(("grp", "pi"), None, None),
            P(("grp", "pi"), None),
            P(("grp", "pi"), None),
            P("grp", None),
            P("grp"),
        ),
        check_vma=False,
    )
```
